32 devices in a mesh: seq: 8 (over z, y), head: 4 (over x, core).
Axes of the slice: x: 2, y: 2, z: 4, core: 2. Of those that a mesh axis runs over, the one named last changes fastest.
Arguments:
- prompt_tokens: bfloat16 [2, 2048, 8192], P(None, ('seq', 'head')), may hold values from -6 to 6
- prompt_write: bfloat16 [2, 2048, 1024], P(None, 'seq', 'head'), may hold values from -0.47851562 to 0.47851562
- prompt_read: bfloat16 [2, 2048, 1024], P(None, 'seq', 'head'), may hold values from -0.47851562 to 0.47851562
- prompt_decay: float32 [2, 128, 2048], P(None, 'head', 'seq'), may hold values from -1 to 0, as said below
- prompt_cotangent: bfloat16 [2, 2048, 8192], P(None, 'seq', 'head'), may hold values from -6 to 6
- answer_tokens: bfloat16 [8, 256, 8192], P('seq', 'head'), may hold values from -6 to 6
- answer_write: bfloat16 [8, 256, 1024], P('seq', None, 'head'), may hold values from -0.47851562 to 0.47851562
- answer_read: bfloat16 [8, 256, 1024], P('seq', None, 'head'), may hold values from -0.47851562 to 0.47851562
- answer_decay: float32 [8, 128, 256], P('seq', 'head'), may hold values from -1 to 0, as said below
- answer_cotangent: bfloat16 [8, 256, 8192], P('seq', None, 'head'), may hold values from -6 to 6
- group_sizes: int32 [2], replicated, may hold values from 2 to 6, as said below
- answer_lengths: int32 [8], P('seq'), may hold values from 1 to 256, 1280 in all
Outputs:
- prompt_output: bfloat16 [2, 2048, 8192], P(None, 'seq', 'head')
- prompt_tokens_adjoint: bfloat16 [2, 2048, 8192], P(None, ('seq', 'head'))
- prompt_write_adjoint: bfloat16 [2, 2048, 1024], P(None, 'seq', 'head')
- prompt_read_adjoint: bfloat16 [2, 2048, 1024], P(None, 'seq', 'head')
- prompt_decay_adjoint: float32 [2, 128, 2048], P(None, 'head', 'seq')
- answer_output: bfloat16 [8, 256, 8192], P('seq', None, 'head')
- answer_tokens_adjoint: bfloat16 [8, 256, 8192], P('seq', 'head')
- answer_write_adjoint: bfloat16 [8, 256, 1024], P('seq', None, 'head')
- answer_read_adjoint: bfloat16 [8, 256, 1024], P('seq', None, 'head')
- answer_decay_adjoint: float32 [8, 128, 256], P('seq', 'head')
The draws below stay inside these ranges and needn't reach their ends.
Inputs may be any that keep to these rules, and one draw needn't show every extreme that they name: Completions are stored in prompt order: the first group_sizes[0] completions follow prompt 0, the next group_sizes[1] prompt 1, and so on; the sizes sum to 8, and one prompt has exactly 6. Completion i has loss and outputs at its first answer_lengths[i] positions only. `prompt_decay`: log decays are negative. `answer_decay`: log decays are negative.
All inputs are finite; a program needn't handle non-finite values. No bound on the sum of `answer_lengths` on one device may be relied on, other than what follows from the above.
Results may differ from the reference program's by a relative error of at most 0.015.
Values may be sent and summed in bfloat16 or wider, within the bound.
A program may use at most 128 MiB of HBM per device.

```python
import math
from functools import partial
import jax
import jax.numpy as jnp
import numpy as np
from jax import lax

HEADS = 128
HEAD_DIM = 64
STATE = 128
GROUPS = 8
BLOCK = 256
PROMPTS = 2
PCH = 256
CLEN = 256
PLEN = 2048
ANSWERS = 8


def decay_law(key, count_of_rows, head_count, total_length, horizon, segment):
    random_subkeys = jax.random.split(key, 7)
    fast_share = 0.5
    fast_heads = jax.random.uniform(random_subkeys[0], (count_of_rows, head_count)) < fast_share
    slow_rate = jnp.exp(jax.random.uniform(random_subkeys[1], (count_of_rows, head_count), minval=jnp.log(0.05), maxval=jnp.log(0.6))) / horizon
    fast_rate = jnp.exp(jax.random.uniform(random_subkeys[2], (count_of_rows, head_count), minval=jnp.log(1.0 / 50.0), maxval=jnp.log(1.0 / 30.0)))
    decay_speed = jnp.where(fast_heads, fast_rate, slow_rate)
    jaggedness = jax.random.uniform(random_subkeys[3], (count_of_rows, head_count, total_length), minval=0.5, maxval=1.5)
    local_region = jnp.exp(jax.random.uniform(random_subkeys[4], (count_of_rows, head_count, total_length // segment), minval=jnp.log(0.7), maxval=jnp.log(1.4)))
    local_region = jnp.repeat(local_region, segment, axis=2)
    spike_events = jax.random.uniform(random_subkeys[5], (count_of_rows, total_length)) < 3.0 / total_length
    magnitude = jax.random.uniform(random_subkeys[6], (count_of_rows, head_count, total_length), minval=0.22, maxval=0.69)
    return -(decay_speed[..., None] * jaggedness * local_region + jnp.where(spike_events[:, None, :], magnitude, 0.0))


def draw_prompt_decay(key, part):
    return decay_law(jax.random.fold_in(key, 11), PROMPTS, HEADS, PLEN, PLEN, PCH).astype(jnp.float32)


def draw_answer_decay(key, part):
    return decay_law(jax.random.fold_in(key, 23), ANSWERS, HEADS, CLEN, CLEN, BLOCK).astype(jnp.float32)


def draw_group_sizes(key, part):
    larger = 3 * ANSWERS // 4
    smaller = ANSWERS - larger
    flipped = jax.random.randint(jax.random.fold_in(key, 37), (), 0, 2)
    first = jnp.where(flipped == 0, larger, smaller)
    second = jnp.where(flipped == 0, smaller, larger)
    return jnp.stack([first, second]).astype(jnp.int32)


def block_levels(key, extent, pieces, low, largest):
    loudness, own = 1.0, jax.random.fold_in(key, 6)
    for position, blocks in pieces:
        steps = jnp.exp(jax.random.uniform(jax.random.fold_in(own, position), (blocks,), jnp.float32, low / len(pieces), largest / len(pieces)))
        loudness = loudness * jnp.repeat(steps, extent[position] // blocks).reshape([-1 if axis == position else 1 for axis in range(len(extent))])
    return loudness


def length_profile(count, total, bound, skew):
    loads = [(1 << 20) // math.isqrt(grade ** skew) + 1 for grade in range(2, count + 1)]
    spare, holding = total - bound - (count - 1), [1] * (count - 1)
    while spare > 0:
        candidates = [i for i in range(count - 1) if holding[i] < bound]
        mass, left = sum([loads[i] for i in candidates]), spare
        for i in candidates:
            more = min(bound - holding[i], max(1, left * loads[i] // mass), spare)
            holding[i] = holding[i] + more
            spare = spare - more
    return np.array([bound] + holding)


def ragged_sizes(rng, count, total, most, lean):
    if count == 2:
        one = jax.random.randint(rng, (), max(1, total - most), min(most, total - 1) + 1)
        return jnp.stack([one, total - one])
    sizes = jnp.asarray(length_profile(count, total, most, lean), jnp.int32)
    twos = (count - 1) // 2
    source_of, receiver = sizes[1:1 + 2 * twos:2], sizes[2:2 + 2 * twos:2]
    slack = jnp.minimum(source_of - 1, most - receiver)
    moved = jax.random.randint(jax.random.fold_in(rng, 1), (twos,), 0, 1 << 20) % (slack + 1)
    sizes = sizes.at[1:1 + 2 * twos:2].set(source_of - moved).at[2:2 + 2 * twos:2].set(receiver + moved)
    return sizes[jax.random.permutation(jax.random.fold_in(rng, 2), count)]


def centred(stream_key, dims, width, reach, pieces=(), kind=jnp.bfloat16):
    array = width * jax.random.normal(stream_key, dims, jnp.float32)
    if pieces:
        array = array * block_levels(stream_key, dims, pieces, -0.22, 0.18)
    return jnp.clip(array, -reach, reach).astype(kind)


def setup_inputs(seed: int = 0) -> dict:
    keys = jax.random.split(jax.random.key(seed), 13)
    prompt_tokens = centred(keys[0], (PROMPTS, PLEN, HEADS * HEAD_DIM), 1.0, 6.0, ((1, 32),))
    prompt_write = centred(keys[1], (PROMPTS, PLEN, GROUPS * STATE), 0.08, 0.47851562, ((1, 8), (2, 4)))
    prompt_read = centred(keys[2], (PROMPTS, PLEN, GROUPS * STATE), 0.08, 0.47851562, ((1, 8), (2, 4)))
    prompt_decay = draw_prompt_decay(jax.random.fold_in(keys[12], 71), 0)
    prompt_cotangent = centred(keys[4], (PROMPTS, PLEN, HEADS * HEAD_DIM), 1.0, 6.0, ((1, 8), (2, 4)))
    answer_tokens = centred(keys[5], (ANSWERS, CLEN, HEADS * HEAD_DIM), 1.0, 6.0, ((0, 8), (1, 4)))
    answer_write = centred(keys[6], (ANSWERS, CLEN, GROUPS * STATE), 0.08, 0.47851562, ((0, 8), (2, 4)))
    answer_read = centred(keys[7], (ANSWERS, CLEN, GROUPS * STATE), 0.08, 0.47851562, ((0, 8), (2, 4)))
    answer_decay = draw_answer_decay(jax.random.fold_in(keys[12], 71), 0)
    answer_cotangent = centred(keys[9], (ANSWERS, CLEN, HEADS * HEAD_DIM), 1.0, 6.0, ((0, 8), (2, 4)))
    group_sizes = draw_group_sizes(jax.random.fold_in(keys[12], 71), 0)
    answer_lengths = ragged_sizes(keys[11], ANSWERS, ANSWERS * CLEN * 5 // 8, CLEN, 1).astype(jnp.int32)
    return {"prompt_tokens": prompt_tokens, "prompt_write": prompt_write, "prompt_read": prompt_read, "prompt_decay": prompt_decay, "prompt_cotangent": prompt_cotangent, "answer_tokens": answer_tokens, "answer_write": answer_write, "answer_read": answer_read, "answer_decay": answer_decay, "answer_cotangent": answer_cotangent, "group_sizes": group_sizes, "answer_lengths": answer_lengths}


def contract(pattern, first_operand, second_operand):
    return jnp.einsum(pattern, first_operand.astype(jnp.float32), second_operand.astype(jnp.float32), precision=lax.Precision.HIGHEST)

def ssd_scan(tokens, key_inputs, query_inputs, log_decay, initial, block_size):
    total_length = tokens.shape[0]
    head_count, state_size, head_size = initial.shape
    groups = key_inputs.shape[1] // state_size
    per_group = head_count // groups
    blocks = total_length // block_size
    values = tokens.reshape(blocks, block_size, groups, per_group, head_size)
    key_rows = key_inputs.reshape(blocks, block_size, groups, state_size)
    queries = query_inputs.reshape(blocks, block_size, groups, state_size)
    running = jnp.cumsum(log_decay.reshape(groups, per_group, blocks, block_size).transpose(2, 0, 1, 3), axis=3)
    closing = running[..., -1]
    scores = contract('cign,cjgn->cgij', queries, key_rows)
    causal = lax.broadcasted_iota(jnp.int32, (block_size, block_size), 0) >= lax.broadcasted_iota(jnp.int32, (block_size, block_size), 1)
    spread = running[..., :, None] - running[..., None, :]
    weights = jnp.where(causal, jnp.exp(jnp.where(causal, spread, 0.0)), 0.0)
    mixing = (weights * scores[:, :, None]).astype(jnp.bfloat16)
    inside = contract('cghij,cjghp->cighp', mixing, values)
    to_close = jnp.exp(closing[..., None] - running).transpose(0, 3, 1, 2)
    weighted = (values.astype(jnp.float32) * to_close[..., None]).astype(jnp.bfloat16)
    block_states = contract('cjgn,cjghp->cghnp', key_rows, weighted)

    def advance(carried, scan_item):
        fresh_state, factor = scan_item
        return (jnp.exp(factor)[..., None, None] * carried + fresh_state, carried)
    ending, starting = lax.scan(advance, initial.reshape(groups, per_group, state_size, head_size), (block_states, closing))
    outside = contract('cign,cghnp->cighp', queries, starting.astype(jnp.bfloat16))
    outside = outside * jnp.exp(running).transpose(0, 3, 1, 2)[..., None]
    output = (inside + outside).reshape(total_length, head_count * head_size)
    return (output, ending.reshape(head_count, state_size, head_size))

def regroup_columns(stacked):
    shape = stacked.shape
    return stacked.transpose(1, 2, 0, 3).reshape(shape[1], shape[2], shape[0] * shape[3])

def regroup_rows(stacked):
    shape = stacked.shape
    return stacked.transpose(1, 0, 2, 3).reshape(shape[1], shape[0] * shape[2], shape[3])

def reference(prompt_tokens, prompt_write, prompt_read, prompt_decay, prompt_cotangent, answer_tokens, answer_write, answer_read, answer_decay, answer_cotangent, group_sizes, answer_lengths):
    per_group = HEADS // GROUPS
    slots = jnp.arange(ANSWERS, dtype=jnp.int32)
    bounds = jnp.cumsum(group_sizes).astype(jnp.int32)
    owner = lax.optimization_barrier(jnp.sum((slots[:, None] >= bounds[None, :]).astype(jnp.int32), axis=1))
    live = jnp.arange(CLEN, dtype=jnp.int32)[None, :] < answer_lengths[:, None]
    answer_seed = jnp.where(live[..., None], answer_cotangent, jnp.zeros_like(answer_cotangent)).astype(jnp.float32)
    prompt_seed = prompt_cotangent.astype(jnp.float32)
    batched = jax.vmap(partial(ssd_scan, block_size=BLOCK))

    def one_group(group_index):
        column = group_index * (per_group * HEAD_DIM)
        state_column = group_index * STATE
        head_row = group_index * per_group
        p_tok = lax.dynamic_slice_in_dim(prompt_tokens, column, per_group * HEAD_DIM, 2)
        p_wri = lax.dynamic_slice_in_dim(prompt_write, state_column, STATE, 2)
        p_rea = lax.dynamic_slice_in_dim(prompt_read, state_column, STATE, 2)
        p_dec = lax.dynamic_slice_in_dim(prompt_decay, head_row, per_group, 1)
        a_tok = lax.dynamic_slice_in_dim(answer_tokens, column, per_group * HEAD_DIM, 2)
        a_wri = lax.dynamic_slice_in_dim(answer_write, state_column, STATE, 2)
        a_rea = lax.dynamic_slice_in_dim(answer_read, state_column, STATE, 2)
        a_dec = lax.dynamic_slice_in_dim(answer_decay, head_row, per_group, 1)

        def forward(tok_one, wri_one, rea_one, dec_one, tok_two, wri_two, rea_two, dec_two):
            blank = jnp.zeros((PROMPTS, per_group, STATE, HEAD_DIM), jnp.float32)
            prompt_result, prompt_end = batched(tok_one, wri_one, rea_one, dec_one, blank)
            answer_start = prompt_end[owner]
            answer_result = batched(tok_two, wri_two, rea_two, dec_two, answer_start)[0]
            return (prompt_result, answer_result)
        results, pull = jax.vjp(forward, p_tok, p_wri, p_rea, p_dec, a_tok, a_wri, a_rea, a_dec)
        seeds = (lax.dynamic_slice_in_dim(prompt_seed, column, per_group * HEAD_DIM, 2), lax.dynamic_slice_in_dim(answer_seed, column, per_group * HEAD_DIM, 2))
        grads = pull(seeds)
        answer_out = jnp.where(live[..., None], results[1], 0.0).astype(jnp.bfloat16)
        return (results[0].astype(jnp.bfloat16), grads[0], grads[1], grads[2], grads[3], answer_out, grads[4], grads[5], grads[6], grads[7])
    stacked = lax.map(one_group, jnp.arange(GROUPS, dtype=jnp.int32))
    return (regroup_columns(stacked[0]), regroup_columns(stacked[1]), regroup_columns(stacked[2]), regroup_columns(stacked[3]), regroup_rows(stacked[4]), regroup_columns(stacked[5]), regroup_columns(stacked[6]), regroup_columns(stacked[7]), regroup_columns(stacked[8]), regroup_rows(stacked[9]))
```

```python
import jax
import jax.numpy as jnp
from jax import lax
from jax.experimental import pallas as pl
from jax.experimental.pallas import tpu as pltpu
from jax.sharding import PartitionSpec as P

HEAD_DIM = 64
STATE = 128
BLOCK = 256
F32 = jnp.float32
BF16 = jnp.bfloat16
NN = (((1,), (0,)), ((), ()))
NT = (((1,), (1,)), ((), ()))
TN = (((0,), (0,)), ((), ()))
PARAMS = pltpu.CompilerParams(vmem_limit_bytes=56 * 1024 * 1024)


def mm(a, b, dims):
    return lax.dot_general(a, b, dims, preferred_element_type=F32)


def mm_exact(a, b, dims):
    return lax.dot_general(a, b, dims, precision=lax.Precision.HIGHEST, preferred_element_type=F32)


def two_term(value):
    high = value.astype(BF16)
    return high, (value - high.astype(F32)).astype(BF16)


def triangle(size, lower=True):
    row = lax.broadcasted_iota(jnp.int32, (size, size), 0)
    column = lax.broadcasted_iota(jnp.int32, (size, size), 1)
    return jnp.where(row >= column if lower else row < column, 1.0, 0.0).astype(F32)


def running_columns(decay):
    return mm_exact(triangle(decay.shape[1]), decay, NT)


def spread_heads(columns, heads):
    row = lax.broadcasted_iota(jnp.int32, (heads, heads * HEAD_DIM), 0)
    lane = lax.broadcasted_iota(jnp.int32, (heads, heads * HEAD_DIM), 1)
    pick = jnp.where(lane // HEAD_DIM == row, 1.0, 0.0).astype(BF16)
    high, low = two_term(columns)
    return mm(high, pick, NN) + mm(low, pick, NN)


def head_sums(value, heads):
    width = value.shape[1]
    row = lax.broadcasted_iota(jnp.int32, (heads, width), 0)
    lane = lax.broadcasted_iota(jnp.int32, (heads, width), 1)
    pick = jnp.where(lane // HEAD_DIM == row, 1.0, 0.0).astype(BF16)
    high, low = two_term(value)
    return mm(pick, high, NT) + mm(pick, low, NT)


def masked_rows(dy, limit):
    row = lax.broadcasted_iota(jnp.int32, dy.shape, 0)
    return jnp.where(row < limit, dy.astype(F32), 0.0)


def start_grad_kernel(limits, dy_ref, read_ref, decay_ref, out_ref):
    heads = decay_ref.shape[1]
    dy = masked_rows(dy_ref[0], limits[pl.program_id(0)])
    er = spread_heads(jnp.exp(running_columns(decay_ref[0])), heads)
    edy = (er * dy).astype(BF16)
    state = mm(read_ref[0], edy, TN)
    out_ref[:, 0] = state.reshape(out_ref.shape[0], out_ref.shape[2], -1).astype(BF16)


def local_end_kernel(x_ref, write_ref, decay_ref, out_ref):
    heads = decay_ref.shape[1]
    x = x_ref[:, 0].reshape(-1, x_ref.shape[3])
    r = running_columns(decay_ref[0])
    ec = spread_heads(jnp.exp(r[-1:] - r), heads)
    w = (ec * x.astype(F32)).astype(BF16)
    state = mm(write_ref[0], w, TN)
    out_ref[:, 0] = state.reshape(out_ref.shape[0], out_ref.shape[2], -1).astype(BF16)


def inside_kernel(
    limits, x_ref, dy_ref, write_ref, read_ref, decay_ref, y_ref, dx_ref, dw_ref, dr_ref, sum_ref, ds_ref, dy_scr
):
    heads = decay_ref.shape[1]
    length = decay_ref.shape[2]
    decay = decay_ref[0]
    write, read = write_ref[0], read_ref[0]
    dy_scr[...] = masked_rows(dy_ref[0], limits[pl.program_id(0)]).astype(BF16)
    tri = triangle(length)
    r_col = mm_exact(tri, decay, NT)
    r_row = mm_exact(decay, tri, NT)
    scores = mm(read, write, NT)
    causal = lax.broadcasted_iota(jnp.int32, (length, length), 0) >= lax.broadcasted_iota(
        jnp.int32, (length, length), 1
    )
    lane = lax.broadcasted_iota(jnp.int32, (1, 2 * HEAD_DIM), 1)
    half = (
        jnp.where(lane < HEAD_DIM, 1.0, 0.0).astype(BF16),
        jnp.where(lane < HEAD_DIM, 0.0, 1.0).astype(BF16),
    )
    sums = jnp.zeros((heads, length), F32)
    row_id = lax.broadcasted_iota(jnp.int32, (heads, 2 * HEAD_DIM), 0)
    lane_id = lax.broadcasted_iota(jnp.int32, (heads, 2 * HEAD_DIM), 1)
    for pair in range(heads // 2):
        columns = slice(pair * 2 * HEAD_DIM, (pair + 1) * 2 * HEAD_DIM)
        x = x_ref[:, 0, :, columns].reshape(length, 2 * HEAD_DIM)
        dy = dy_scr[:, columns]
        y = jnp.zeros((length, 2 * HEAD_DIM), F32)
        dx = jnp.zeros((length, 2 * HEAD_DIM), F32)
        for one in range(2):
            head = pair * 2 + one
            x_one, dy_one = x * half[one], dy * half[one]
            gap = r_col[:, head : head + 1] - r_row[head : head + 1, :]
            weights = jnp.exp(jnp.where(causal, gap, -1e30))
            mixing = (weights * scores).astype(BF16)
            y = y + mm(mixing, x_one, NN)
            dx = dx + mm(mixing, dy_one, TN)
            pulled = mm(dy_one, x, NT) * weights
            if head == 0:
                ds_ref[...] = pulled
            else:
                ds_ref[...] += pulled
        y_ref[0, :, columns] = y.astype(BF16)
        dx_ref[:, 0, :, columns] = dx.astype(BF16).reshape(dx_ref.shape[0], dx_ref.shape[2], 2 * HEAD_DIM)
        pick = jnp.where(row_id == 2 * pair + lane_id // HEAD_DIM, 1.0, 0.0).astype(BF16)
        high, low = two_term(dy.astype(F32) * y - x.astype(F32) * dx)
        sums = sums + mm(pick, high, NT) + mm(pick, low, NT)
    sum_ref[0] = sums
    ds = ds_ref[...].astype(BF16)
    dr_ref[0] = mm(ds, write, NN).astype(dr_ref.dtype)
    dw_ref[0] = mm(ds, read, TN).astype(dw_ref.dtype)


def chain_kernel(owner, recv_ref, out_ref, *, prompts, answers):
    devices = recv_ref.shape[0]

    def part(source, slot):
        return recv_ref[source, slot].astype(F32)

    def factor(source, prompt):
        slot = 2 * prompts + answers
        high = recv_ref[source, slot, 2 * prompt : 2 * prompt + 1, :].astype(F32)
        low = recv_ref[source, slot, 2 * prompt + 1 : 2 * prompt + 2, :].astype(F32)
        return high + low

    finals = []
    for prompt in range(prompts):
        carried = jnp.zeros(recv_ref.shape[2:], F32)
        for source in range(devices):
            out_ref[source, prompt] = carried.astype(BF16)
            carried = factor(source, prompt) * carried + part(source, prompt)
        finals.append(carried)
    for source in range(devices):
        for answer in range(answers):
            mine = owner[source * answers + answer]
            chosen = finals[0]
            for prompt in range(1, prompts):
                chosen = jnp.where(mine == prompt, finals[prompt], chosen)
            out_ref[source, 2 * prompts + answer] = chosen.astype(BF16)
    for prompt in range(prompts):
        carried = jnp.zeros(recv_ref.shape[2:], F32)
        for source in range(devices):
            for answer in range(answers):
                mine = owner[source * answers + answer]
                carried = carried + jnp.where(mine == prompt, part(source, 2 * prompts + answer), 0.0)
        for source in range(devices - 1, -1, -1):
            out_ref[source, prompts + prompt] = carried.astype(BF16)
            carried = factor(source, prompt) * carried + part(source, prompts + prompt)


def state_of(ref):
    value = ref[:, 0].astype(F32)
    return value.reshape(STATE, value.shape[2]).astype(BF16)


def reverse_sums(value):
    return mm_exact(value, triangle(value.shape[1]), NN)


def prompt_final_kernel(
    start_ref, grad_ref, x_ref, dy_ref, write_ref, read_ref, decay_ref, yin_ref, dxin_ref, dwin_ref, drin_ref, sumin_ref,
    y_ref, dx_ref, dw_ref, dr_ref, dd_ref,
):
    heads = decay_ref.shape[1]
    start, grad = state_of(start_ref), state_of(grad_ref)
    x = x_ref[:, 0].reshape(-1, x_ref.shape[3])
    dy = dy_ref[0].astype(F32)
    write, read = write_ref[0], read_ref[0]
    r = running_columns(decay_ref[0])
    er = spread_heads(jnp.exp(r), heads)
    outside = er * mm(read, start, NN)
    y_ref[0] = (yin_ref[0].astype(F32) + outside).astype(BF16)
    dr_ref[0] = (drin_ref[0] + mm((er * dy).astype(BF16), start, NT)).astype(BF16)
    sums = sumin_ref[0] + head_sums(dy * outside, heads)
    ec = spread_heads(jnp.exp(r[-1:] - r), heads)
    xf = x.astype(F32)
    dw_ref[0] = (dwin_ref[0] + mm((ec * xf).astype(BF16), grad, NT)).astype(BF16)
    moved = ec * mm(write, grad, NN)
    dx_in = dxin_ref[:, 0].reshape(x.shape).astype(F32)
    dx_ref[:, 0] = (dx_in + moved).astype(BF16).reshape(dx_ref.shape[0], dx_ref.shape[2], dx_ref.shape[3])
    pulled = head_sums(xf * moved, heads)
    kept = head_sums(start.astype(F32) * grad.astype(F32), heads)
    closing = jnp.exp(jnp.sum(decay_ref[0], axis=1, keepdims=True)) * jnp.sum(kept, axis=1, keepdims=True)
    size = sums.shape[1]
    dd_ref[0] = reverse_sums(sums) + mm_exact(pulled, triangle(size, False), NN) + closing


def answer_final_kernel(
    limits, start_ref, dy_ref, read_ref, decay_ref, yin_ref, drin_ref, sumin_ref, y_ref, dr_ref, dd_ref
):
    heads = decay_ref.shape[1]
    limit = limits[pl.program_id(0)]
    start = state_of(start_ref)
    dy = masked_rows(dy_ref[0], limit)
    er = spread_heads(jnp.exp(running_columns(decay_ref[0])), heads)
    outside = er * mm(read_ref[0], start, NN)
    y_ref[0] = masked_rows(yin_ref[0].astype(F32) + outside, limit).astype(BF16)
    dr_ref[0] = (drin_ref[0] + mm((er * dy).astype(BF16), start, NT)).astype(BF16)
    dd_ref[0] = reverse_sums(sumin_ref[0] + head_sums(dy * outside, heads))


def per_device(
    prompt_tokens,
    prompt_write,
    prompt_read,
    prompt_decay,
    prompt_cotangent,
    answer_tokens,
    answer_write,
    answer_read,
    answer_decay,
    answer_cotangent,
    group_sizes,
    answer_lengths,
):
    prompts, local_heads, length = prompt_decay.shape
    answers = answer_decay.shape[0]
    groups = prompt_write.shape[2] // STATE
    heads = local_heads // groups
    devices = lax.axis_size("seq")
    split = lax.axis_size("head")
    width, columns = heads * HEAD_DIM, local_heads * HEAD_DIM
    rows, piece = STATE // devices, length // split
    assert length == BLOCK and answer_decay.shape[2] == length

    token = pl.BlockSpec((split, 1, piece, width), lambda s, g, *_: (0, s, 0, g))
    wide = pl.BlockSpec((1, length, width), lambda s, g, *_: (s, 0, g))
    narrow = pl.BlockSpec((1, length, STATE), lambda s, g, *_: (s, 0, g))
    perhead = pl.BlockSpec((1, heads, length), lambda s, g, *_: (s, g, 0))

    def token_at(first):
        return pl.BlockSpec((split, 1, piece, width), lambda s, g, *_: (0, s + first, 0, g))

    def state_at(first):
        return pl.BlockSpec((devices, 1, rows, width), lambda s, g, *_: (0, s + first, 0, g))

    def shape(dims, kind=BF16):
        return jax.ShapeDtypeStruct(dims, kind)

    def call(kernel, count, prefetch, ins, outs, out_shape, name, flops, scratch=(), grid=None):
        return pl.pallas_call(
            kernel,
            grid_spec=pltpu.PrefetchScalarGridSpec(
                num_scalar_prefetch=prefetch,
                grid=grid or (count, groups),
                in_specs=ins,
                out_specs=outs,
                scratch_shapes=list(scratch),
            ),
            out_shape=out_shape,
            compiler_params=PARAMS,
            name=name,
            cost_estimate=pl.CostEstimate(
                flops=flops * count, bytes_accessed=flops * count // 200, transcendentals=0
            ),
        )

    whole = jnp.full((prompts,), length, jnp.int32)
    stacked = jnp.concatenate([prompt_tokens, answer_tokens], axis=0)
    sequences = prompts + answers
    stacked = stacked.reshape(sequences, piece, split, columns).transpose(2, 0, 1, 3)
    x = lax.all_to_all(stacked, "head", split_axis=0, concat_axis=0, tiled=True)

    state_flops = 2 * length * STATE * columns

    def start_grad(count, limits, dy, read, decay, name):
        return call(
            start_grad_kernel, count, 1, [wide, narrow, perhead], state_at(0),
            shape((devices, count, rows, columns)), name, state_flops,
        )(limits, dy, read, decay)

    grad_prompt = start_grad(prompts, whole, prompt_cotangent, prompt_read, prompt_decay, "grad_prompt")
    grad_answer = start_grad(answers, answer_lengths, answer_cotangent, answer_read, answer_decay, "grad_answer")
    end_prompt = call(
        local_end_kernel, prompts, 0, [token_at(0), narrow, perhead], state_at(0),
        shape((devices, prompts, rows, columns)), "end_prompt", state_flops,
    )(x, prompt_write, prompt_decay)

    total = jnp.exp(jnp.sum(prompt_decay, axis=2))
    total_high, total_low = two_term(total)
    pieces = jnp.stack([total_high, total_low], axis=1).reshape(2 * prompts, local_heads)
    pieces = jnp.repeat(pieces, HEAD_DIM, axis=1)
    pieces = jnp.pad(pieces, ((0, rows - 2 * prompts), (0, 0)))
    pieces = jnp.broadcast_to(pieces[None, None], (devices, 1, rows, columns))
    sent = jnp.concatenate([end_prompt, grad_prompt, grad_answer, pieces], axis=1)
    received = lax.all_to_all(sent, "seq", split_axis=0, concat_axis=0, tiled=True)

    def inside(count, limits, first, dy, write, read, decay, kind, name):
        return call(
            inside_kernel, count, 1, [token_at(first), wide, narrow, narrow, perhead],
            [wide, token, narrow, narrow, perhead],
            [
                shape((count, length, columns)),
                shape((split, count, piece, columns)),
                shape((count, length, groups * STATE), kind),
                shape((count, length, groups * STATE), F32),
                shape((count, local_heads, length), F32),
            ],
            name, 8 * length * length * columns,
            (pltpu.VMEM((length, length), F32), pltpu.VMEM((length, width), BF16)),
        )(limits, x, dy, write, read, decay)

    p_y, p_dx, p_dw, p_dr, p_sum = inside(
        prompts, whole, 0, prompt_cotangent, prompt_write, prompt_read, prompt_decay, F32, "inside_prompt"
    )
    a_y, a_dx, a_dw, a_dr, a_sum = inside(
        answers, answer_lengths, prompts, answer_cotangent, answer_write, answer_read, answer_decay, BF16,
        "inside_answer",
    )

    slots = jnp.arange(devices * answers, dtype=jnp.int32)
    bounds = jnp.cumsum(group_sizes)
    owner = jnp.sum((slots[:, None] >= bounds[None, :]).astype(jnp.int32), axis=1)
    states = 2 * prompts + answers
    lanes = 512 if columns % 512 == 0 else columns

    def chain(owner_ref, recv_ref, out_ref):
        chain_kernel(owner_ref, recv_ref, out_ref, prompts=prompts, answers=answers)

    replies = call(
        chain, 1, 1,
        [pl.BlockSpec((devices, states + 1, rows, lanes), lambda c, *_: (0, 0, 0, c))],
        pl.BlockSpec((devices, states, rows, lanes), lambda c, *_: (0, 0, 0, c)),
        shape((devices, states, rows, columns)), "chain", state_flops // 8, (), (columns // lanes,),
    )(owner, received)
    carried = lax.all_to_all(replies, "seq", split_axis=0, concat_axis=0, tiled=True)

    prompt_output, dx, prompt_dw, prompt_dr, prompt_dd = call(
        prompt_final_kernel, prompts, 0,
        [state_at(0), state_at(prompts), token_at(0), wide, narrow, narrow, perhead,
         wide, token, narrow, narrow, perhead],
        [wide, token, narrow, narrow, perhead],
        [
            shape((prompts, length, columns)),
            shape((split, prompts, piece, columns)),
            shape((prompts, length, groups * STATE)),
            shape((prompts, length, groups * STATE)),
            shape((prompts, local_heads, length), F32),
        ],
        "prompt_final", 4 * state_flops,
    )(carried, carried, x, prompt_cotangent, prompt_write, prompt_read, prompt_decay, p_y, p_dx, p_dw, p_dr, p_sum)
    answer_output, answer_dr, answer_dd = call(
        answer_final_kernel, answers, 1,
        [state_at(2 * prompts), wide, narrow, perhead, wide, narrow, perhead],
        [wide, narrow, perhead],
        [
            shape((answers, length, columns)),
            shape((answers, length, groups * STATE)),
            shape((answers, local_heads, length), F32),
        ],
        "answer_final", 2 * state_flops,
    )(answer_lengths, carried, answer_cotangent, answer_read, answer_decay, a_y, a_dr, a_sum)

    def token_back(value):
        back = lax.all_to_all(value, "head", split_axis=0, concat_axis=0, tiled=True)
        return back.transpose(1, 2, 0, 3).reshape(value.shape[1], piece, split * columns)

    return (
        prompt_output,
        token_back(dx),
        prompt_dw,
        prompt_dr,
        prompt_dd,
        answer_output,
        token_back(a_dx),
        a_dw,
        answer_dr,
        answer_dd,
    )


def solution(mesh):
    return jax.shard_map(
        per_device,
        mesh=mesh,
        in_specs=(
            P(None, ("seq", "head"), None),
            P(None, "seq", "head"),
            P(None, "seq", "head"),
            P(None, "head", "seq"),
            P(None, "seq", "head"),
            P("seq", "head", None),
            P("seq", None, "head"),
            P("seq", None, "head"),
            P("seq", "head", None),
            P("seq", None, "head"),
            P(),
            P("seq"),
        ),
        out_specs=(
            P(None, "seq", "head"),
            P(None, ("seq", "head"), None),
            P(None, "seq", "head"),
            P(None, "seq", "head"),
            P(None, "head", "seq"),
            P("seq", None, "head"),
            P("seq", "head", None),
            P("seq", None, "head"),
            P("seq", None, "head"),
            P("seq", "head", None),
        ),
        check_vma=False,
    )
```

```python
from functools import partial

import jax
import jax.numpy as jnp
from jax import lax
from jax.experimental import pallas as pl
from jax.experimental.pallas import tpu as pltpu
from jax.sharding import PartitionSpec as P

HEAD_DIM = 64
STATE = 128
BLOCK = 256
F32 = jnp.float32
BF16 = jnp.bfloat16
NN = (((1,), (0,)), ((), ()))
NT = (((1,), (1,)), ((), ()))
TN = (((0,), (0,)), ((), ()))
PARAMS = pltpu.CompilerParams(vmem_limit_bytes=56 * 1024 * 1024)


def mm(a, b, dims):
    return lax.dot_general(a, b, dims, preferred_element_type=F32)


def mm_exact(a, b, dims):
    return lax.dot_general(a, b, dims, precision=lax.Precision.HIGHEST, preferred_element_type=F32)


def two_term(value):
    high = value.astype(BF16)
    return high, (value - high.astype(F32)).astype(BF16)


def triangle(size, lower=True):
    row = lax.broadcasted_iota(jnp.int32, (size, size), 0)
    column = lax.broadcasted_iota(jnp.int32, (size, size), 1)
    return jnp.where(row >= column if lower else row < column, 1.0, 0.0).astype(F32)


def running_columns(decay):
    return mm_exact(triangle(decay.shape[1]), decay, NT)


def spread_heads(columns, heads):
    row = lax.broadcasted_iota(jnp.int32, (heads, heads * HEAD_DIM), 0)
    lane = lax.broadcasted_iota(jnp.int32, (heads, heads * HEAD_DIM), 1)
    pick = jnp.where(lane // HEAD_DIM == row, 1.0, 0.0).astype(BF16)
    high, low = two_term(columns)
    return mm(high, pick, NN) + mm(low, pick, NN)


def head_sums(value, heads):
    width = value.shape[1]
    row = lax.broadcasted_iota(jnp.int32, (heads, width), 0)
    lane = lax.broadcasted_iota(jnp.int32, (heads, width), 1)
    pick = jnp.where(lane // HEAD_DIM == row, 1.0, 0.0).astype(BF16)
    high, low = two_term(value)
    return mm(pick, high, NT) + mm(pick, low, NT)


def masked_rows(dy, limit):
    row = lax.broadcasted_iota(jnp.int32, dy.shape, 0)
    return jnp.where(row < limit, dy.astype(F32), 0.0)


def deal_rows(state, place, outs, scratch):
    scratch[...] = state.reshape(scratch.shape)
    for k, out in enumerate(outs):
        out[0] = scratch[place ^ k].astype(BF16)


def start_grad_kernel(limits, place, dy_ref, read_ref, decay_ref, *rest):
    heads = decay_ref.shape[1]
    dy = masked_rows(dy_ref[0], limits[pl.program_id(0)])
    er = spread_heads(jnp.exp(running_columns(decay_ref[0])), heads)
    edy = (er * dy).astype(BF16)
    deal_rows(mm(read_ref[0], edy, TN), place[0], rest[:-1], rest[-1])


def local_end_kernel(place, x_ref, write_ref, decay_ref, *rest):
    heads = decay_ref.shape[1]
    x = x_ref[:, 0].reshape(-1, x_ref.shape[3])
    r = running_columns(decay_ref[0])
    ec = spread_heads(jnp.exp(r[-1:] - r), heads)
    w = (ec * x.astype(F32)).astype(BF16)
    deal_rows(mm(write_ref[0], w, TN), place[0], rest[:-1], rest[-1])


def inside_kernel(
    limits, x_ref, dy_ref, write_ref, read_ref, decay_ref, y_ref, dx_ref, dw_ref, dr_ref, sum_ref, ds_ref, dy_scr
):
    heads = decay_ref.shape[1]
    length = decay_ref.shape[2]
    decay = decay_ref[0]
    write, read = write_ref[0], read_ref[0]
    dy_scr[...] = masked_rows(dy_ref[0], limits[pl.program_id(0)]).astype(BF16)
    tri = triangle(length)
    r_col = mm_exact(tri, decay, NT)
    r_row = mm_exact(decay, tri, NT)
    scores = mm(read, write, NT)
    causal = lax.broadcasted_iota(jnp.int32, (length, length), 0) >= lax.broadcasted_iota(
        jnp.int32, (length, length), 1
    )
    lane = lax.broadcasted_iota(jnp.int32, (1, 2 * HEAD_DIM), 1)
    half = (
        jnp.where(lane < HEAD_DIM, 1.0, 0.0).astype(BF16),
        jnp.where(lane < HEAD_DIM, 0.0, 1.0).astype(BF16),
    )
    sums = jnp.zeros((heads, length), F32)
    row_id = lax.broadcasted_iota(jnp.int32, (heads, 2 * HEAD_DIM), 0)
    lane_id = lax.broadcasted_iota(jnp.int32, (heads, 2 * HEAD_DIM), 1)
    for pair in range(heads // 2):
        columns = slice(pair * 2 * HEAD_DIM, (pair + 1) * 2 * HEAD_DIM)
        x = x_ref[:, 0, :, columns].reshape(length, 2 * HEAD_DIM)
        dy = dy_scr[:, columns]
        y = jnp.zeros((length, 2 * HEAD_DIM), F32)
        dx = jnp.zeros((length, 2 * HEAD_DIM), F32)
        for one in range(2):
            head = pair * 2 + one
            x_one, dy_one = x * half[one], dy * half[one]
            gap = r_col[:, head : head + 1] - r_row[head : head + 1, :]
            weights = jnp.exp(jnp.where(causal, gap, -1e30))
            mixing = (weights * scores).astype(BF16)
            y = y + mm(mixing, x_one, NN)
            dx = dx + mm(mixing, dy_one, TN)
            pulled = mm(dy_one, x, NT) * weights
            if head == 0:
                ds_ref[...] = pulled
            else:
                ds_ref[...] += pulled
        y_ref[0, :, columns] = y.astype(BF16)
        dx_ref[:, 0, :, columns] = dx.astype(BF16).reshape(dx_ref.shape[0], dx_ref.shape[2], 2 * HEAD_DIM)
        pick = jnp.where(row_id == 2 * pair + lane_id // HEAD_DIM, 1.0, 0.0).astype(BF16)
        high, low = two_term(dy.astype(F32) * y - x.astype(F32) * dx)
        sums = sums + mm(pick, high, NT) + mm(pick, low, NT)
    sum_ref[0] = sums
    ds = ds_ref[...].astype(BF16)
    dr_ref[0] = mm(ds, write, NN).astype(dr_ref.dtype)
    dw_ref[0] = mm(ds, read, TN).astype(dw_ref.dtype)


class Side:
    def __init__(self, owner, place, total_ref, ends, grads, seeds, held, prompts, answers):
        half = len(ends)
        self.half, self.prompts, self.answers = half, prompts, answers
        self.owner, self.side = owner, place[1]
        self.total_ref, self.held = total_ref, held
        for k in range(half):
            spot = place[0] ^ k
            held[spot, :prompts] = ends[k][...].astype(F32)
            held[spot, prompts : 2 * prompts] = grads[k][...].astype(F32)
            held[spot, 2 * prompts :] = seeds[k][...].astype(F32)

    def factor(self, j, prompt, side=None):
        side = self.side if side is None else side
        return self.total_ref[side * self.half + j, prompt : prompt + 1, :]

    def forward(self, prompt, carried, out=None):
        for j in range(self.half):
            if out is not None:
                out[j, prompt] = carried
            carried = self.factor(j, prompt) * carried + self.held[j, prompt]
        return carried

    def backward(self, prompt, carried, out=None):
        for j in range(self.half - 1, -1, -1):
            if out is not None:
                out[j, self.prompts + prompt] = carried
            carried = self.factor(j, prompt) * carried + self.held[j, self.prompts + prompt]
        return carried

    def owner_of(self, j, answer):
        return self.owner[(self.side * self.half + j) * self.answers + answer]

    def seed(self, prompt):
        carried = jnp.zeros(self.held.shape[2:], F32)
        for j in range(self.half):
            for answer in range(self.answers):
                mine = self.held[j, 2 * self.prompts + answer]
                carried = carried + jnp.where(self.owner_of(j, answer) == prompt, mine, 0.0)
        return carried


def meet_kernel(owner, place, total_ref, *rest, half, prompts, answers):
    ends, grads, seeds = rest[:half], rest[half : 2 * half], rest[2 * half : 3 * half]
    out_ref, held = rest[3 * half :]
    here = Side(owner, place, total_ref, ends, grads, seeds, held, prompts, answers)
    blank = jnp.zeros(held.shape[2:], F32)
    for prompt in range(prompts):
        out_ref[prompt] = here.forward(prompt, blank).astype(BF16)
        seed = here.seed(prompt)
        folded = here.backward(prompt, seed)
        out_ref[prompts + prompt] = jnp.where(here.side == 1, folded, seed).astype(BF16)


def chain_kernel(owner, place, total_ref, met_ref, *rest, half, prompts, answers):
    ends, grads, seeds = rest[:half], rest[half : 2 * half], rest[2 * half : 3 * half]
    outs, held, done = rest[3 * half : 4 * half], rest[4 * half], rest[4 * half + 1]
    here = Side(owner, place, total_ref, ends, grads, seeds, held, prompts, answers)
    finals = []
    for prompt in range(prompts):
        other = met_ref[prompt].astype(F32)
        beyond = here.factor(0, prompt, 1)
        for j in range(1, half):
            beyond = beyond * here.factor(j, prompt, 1)
        last = here.forward(prompt, jnp.where(here.side == 1, other, 0.0), done)
        finals.append(jnp.where(here.side == 1, last, beyond * last + other))
        pull = met_ref[prompts + prompt].astype(F32)
        scale = jnp.where(here.side == 1, jnp.ones_like(beyond), beyond)
        here.backward(prompt, pull + scale * here.seed(prompt), done)
    for j in range(half):
        for answer in range(answers):
            mine = here.owner_of(j, answer)
            chosen = finals[0]
            for prompt in range(1, prompts):
                chosen = jnp.where(mine == prompt, finals[prompt], chosen)
            done[j, 2 * prompts + answer] = chosen
    for k in range(half):
        outs[k][...] = done[place[0] ^ k].astype(BF16)


def gather_rows(place, refs, scratch):
    for k, ref in enumerate(refs):
        scratch[place ^ k] = ref[0].astype(F32)
    return scratch[...].reshape(STATE, scratch.shape[2]).astype(BF16)


def reverse_sums(value):
    return mm_exact(value, triangle(value.shape[1]), NN)


def prompt_final_kernel(place, *refs, half):
    (
        x_ref, dy_ref, write_ref, read_ref, decay_ref, yin_ref, dxin_ref, dwin_ref, drin_ref, sumin_ref,
        y_ref, dx_ref, dw_ref, dr_ref, dd_ref, scratch,
    ) = refs[2 * half :]
    heads = decay_ref.shape[1]
    start = gather_rows(place[0], refs[:half], scratch)
    grad = gather_rows(place[0], refs[half : 2 * half], scratch)
    x = x_ref[:, 0].reshape(-1, x_ref.shape[3])
    dy = dy_ref[0].astype(F32)
    write, read = write_ref[0], read_ref[0]
    r = running_columns(decay_ref[0])
    er = spread_heads(jnp.exp(r), heads)
    outside = er * mm(read, start, NN)
    y_ref[0] = (yin_ref[0].astype(F32) + outside).astype(BF16)
    dr_ref[0] = (drin_ref[0] + mm((er * dy).astype(BF16), start, NT)).astype(BF16)
    sums = sumin_ref[0] + head_sums(dy * outside, heads)
    ec = spread_heads(jnp.exp(r[-1:] - r), heads)
    xf = x.astype(F32)
    dw_ref[0] = (dwin_ref[0] + mm((ec * xf).astype(BF16), grad, NT)).astype(BF16)
    moved = ec * mm(write, grad, NN)
    dx_in = dxin_ref[:, 0].reshape(x.shape).astype(F32)
    dx_ref[:, 0] = (dx_in + moved).astype(BF16).reshape(dx_ref.shape[0], dx_ref.shape[2], dx_ref.shape[3])
    pulled = head_sums(xf * moved, heads)
    kept = head_sums(start.astype(F32) * grad.astype(F32), heads)
    closing = jnp.exp(jnp.sum(decay_ref[0], axis=1, keepdims=True)) * jnp.sum(kept, axis=1, keepdims=True)
    size = sums.shape[1]
    dd_ref[0] = reverse_sums(sums) + mm_exact(pulled, triangle(size, False), NN) + closing


def answer_final_kernel(limits, place, *refs, half):
    dy_ref, read_ref, decay_ref, yin_ref, drin_ref, sumin_ref, y_ref, dr_ref, dd_ref, scratch = refs[half:]
    heads = decay_ref.shape[1]
    limit = limits[pl.program_id(0)]
    start = gather_rows(place[0], refs[:half], scratch)
    dy = masked_rows(dy_ref[0], limit)
    er = spread_heads(jnp.exp(running_columns(decay_ref[0])), heads)
    outside = er * mm(read_ref[0], start, NN)
    y_ref[0] = masked_rows(yin_ref[0].astype(F32) + outside, limit).astype(BF16)
    dr_ref[0] = (drin_ref[0] + mm((er * dy).astype(BF16), start, NT)).astype(BF16)
    dd_ref[0] = reverse_sums(sumin_ref[0] + head_sums(dy * outside, heads))


def per_device(
    prompt_tokens,
    prompt_write,
    prompt_read,
    prompt_decay,
    prompt_cotangent,
    answer_tokens,
    answer_write,
    answer_read,
    answer_decay,
    answer_cotangent,
    group_sizes,
    answer_lengths,
):
    prompts, local_heads, length = prompt_decay.shape
    answers = answer_decay.shape[0]
    groups = prompt_write.shape[2] // STATE
    heads = local_heads // groups
    devices = lax.axis_size("seq")
    split = lax.axis_size("head")
    half = devices // 2
    position = lax.axis_index("seq")
    width, columns = heads * HEAD_DIM, local_heads * HEAD_DIM
    rows, piece = STATE // half, length // split
    assert length == BLOCK and answer_decay.shape[2] == length
    assert half & (half - 1) == 0

    token = pl.BlockSpec((split, 1, piece, width), lambda s, g, *_: (0, s, 0, g))
    wide = pl.BlockSpec((1, length, width), lambda s, g, *_: (s, 0, g))
    narrow = pl.BlockSpec((1, length, STATE), lambda s, g, *_: (s, 0, g))
    perhead = pl.BlockSpec((1, heads, length), lambda s, g, *_: (s, g, 0))

    def state_at(first):
        return [pl.BlockSpec((1, rows, width), lambda s, g, *_: (s + first, 0, g))] * half

    def shape(dims, kind=BF16):
        return jax.ShapeDtypeStruct(dims, kind)

    def call(kernel, count, prefetch, ins, outs, out_shape, name, flops, scratch=(), grid=None):
        return pl.pallas_call(
            kernel,
            grid_spec=pltpu.PrefetchScalarGridSpec(
                num_scalar_prefetch=prefetch,
                grid=grid or (count, groups),
                in_specs=ins,
                out_specs=outs,
                scratch_shapes=list(scratch),
            ),
            out_shape=out_shape,
            compiler_params=PARAMS,
            name=name,
            cost_estimate=pl.CostEstimate(
                flops=flops * count, bytes_accessed=flops * count // 200, transcendentals=0
            ),
        )

    def after(value, *others):
        return lax.optimization_barrier((value,) + others)[0]

    def deal(parts):
        return [parts[0]] + [
            lax.ppermute(parts[k], "seq", [(d, d ^ k) for d in range(devices)]) for k in range(1, half)
        ]

    def token_out(tokens):
        count = tokens.shape[0]
        packed = tokens.reshape(count, piece, split, columns).transpose(2, 0, 1, 3)
        return lax.all_to_all(packed, "head", split_axis=0, concat_axis=0, tiled=True)

    whole = jnp.full((prompts,), length, jnp.int32)
    place = jnp.stack([position % half, position // half]).astype(jnp.int32)
    state_flops = 2 * length * STATE * columns
    rows_scratch = (pltpu.VMEM((half, rows, width), F32),)

    p_x = token_out(prompt_tokens)

    total = jnp.repeat(jnp.exp(jnp.sum(prompt_decay, axis=2)), HEAD_DIM, axis=1)

    def start_grad(count, limits, dy, read, decay, name):
        return call(
            start_grad_kernel, count, 2, [wide, narrow, perhead], state_at(0),
            [shape((count, rows, columns))] * half, name, state_flops, rows_scratch,
        )(limits, place, dy, read, decay)

    grads = deal(start_grad(prompts, whole, prompt_cotangent, prompt_read, prompt_decay, "grad_prompt"))
    seeds = deal(start_grad(answers, answer_lengths, answer_cotangent, answer_read, answer_decay, "grad_answer"))
    a_x = token_out(after(answer_tokens, grads[0], seeds[0]))
    totals = lax.all_to_all(
        jnp.broadcast_to(after(total, grads[0])[None], (devices, prompts, columns)), "seq", split_axis=0, concat_axis=0, tiled=True
    )
    local_ends = call(
        local_end_kernel, prompts, 1, [token, narrow, perhead], state_at(0),
        [shape((prompts, rows, columns))] * half, "end_prompt", state_flops, rows_scratch,
    )(place, p_x, prompt_write, prompt_decay)
    ends = deal(local_ends)

    def inside(count, limits, x, dy, write, read, decay, kind, name):
        return call(
            inside_kernel, count, 1, [token, wide, narrow, narrow, perhead],
            [wide, token, narrow, narrow, perhead],
            [
                shape((count, length, columns)),
                shape((split, count, piece, columns)),
                shape((count, length, groups * STATE), kind),
                shape((count, length, groups * STATE), F32),
                shape((count, local_heads, length), F32),
            ],
            name, 8 * length * length * columns,
            (pltpu.VMEM((length, length), F32), pltpu.VMEM((length, width), BF16)),
        )(limits, x, dy, write, read, decay)

    p_y, p_dx, p_dw, p_dr, p_sum = inside(
        prompts, after(whole, local_ends[0]), p_x, prompt_cotangent, prompt_write, prompt_read, prompt_decay, F32,
        "inside_prompt",
    )

    slots = jnp.arange(devices * answers, dtype=jnp.int32)
    bounds = jnp.cumsum(group_sizes)
    owner = jnp.sum((slots[:, None] >= bounds[None, :]).astype(jnp.int32), axis=1)
    states = 2 * prompts + answers
    lanes = 512 if columns % 512 == 0 else columns

    def strip(*dims):
        return pl.BlockSpec(dims + (lanes,), lambda c, *_: (0,) * len(dims) + (c,))

    held = pltpu.VMEM((half, states, rows, lanes), F32)
    given = [strip(prompts, rows)] * (2 * half) + [strip(answers, rows)] * half
    sizes = dict(half=half, prompts=prompts, answers=answers)
    meeting = call(
        partial(meet_kernel, **sizes), 1, 2, [strip(devices, prompts)] + given, strip(2 * prompts, rows),
        shape((2 * prompts, rows, columns)), "meet", state_flops // 8, (held,), (columns // lanes,),
    )(after(owner, p_sum), place, totals, *ends, *grads, *seeds)
    met = lax.ppermute(meeting, "seq", [(d, (d + half) % devices) for d in range(devices)])

    a_y, a_dx, a_dw, a_dr, a_sum = inside(
        answers, after(answer_lengths, meeting), a_x, answer_cotangent, answer_write, answer_read, answer_decay, BF16,
        "inside_answer",
    )

    replies = call(
        partial(chain_kernel, **sizes), 1, 2, [strip(devices, prompts), strip(2 * prompts, rows)] + given,
        [strip(states, rows)] * half,
        [shape((states, rows, columns))] * half, "chain", state_flops // 8, (held, held), (columns // lanes,),
    )(after(owner, a_sum), place, totals, met, *ends, *grads, *seeds)
    carried = deal(replies)

    prompt_output, dx, prompt_dw, prompt_dr, prompt_dd = call(
        partial(prompt_final_kernel, half=half), prompts, 1,
        state_at(0) + state_at(prompts)
        + [token, wide, narrow, narrow, perhead, wide, token, narrow, narrow, perhead],
        [wide, token, narrow, narrow, perhead],
        [
            shape((prompts, length, columns)),
            shape((split, prompts, piece, columns)),
            shape((prompts, length, groups * STATE)),
            shape((prompts, length, groups * STATE)),
            shape((prompts, local_heads, length), F32),
        ],
        "prompt_final", 4 * state_flops, rows_scratch,
    )(place, *carried, *carried, p_x, prompt_cotangent, prompt_write, prompt_read, prompt_decay, p_y, p_dx, p_dw, p_dr, p_sum)
    answer_output, answer_dr, answer_dd = call(
        partial(answer_final_kernel, half=half), answers, 2,
        state_at(2 * prompts) + [wide, narrow, perhead, wide, narrow, perhead],
        [wide, narrow, perhead],
        [
            shape((answers, length, columns)),
            shape((answers, length, groups * STATE)),
            shape((answers, local_heads, length), F32),
        ],
        "answer_final", 2 * state_flops, rows_scratch,
    )(answer_lengths, place, *carried, answer_cotangent, answer_read, answer_decay, a_y, a_dr, a_sum)

    def token_back(value):
        back = lax.all_to_all(value, "head", split_axis=0, concat_axis=0, tiled=True)
        return back.transpose(1, 2, 0, 3).reshape(value.shape[1], piece, split * columns)

    return (
        prompt_output,
        token_back(dx),
        prompt_dw,
        prompt_dr,
        prompt_dd,
        answer_output,
        token_back(a_dx),
        a_dw,
        answer_dr,
        answer_dd,
    )


def solution(mesh):
    return jax.shard_map(
        per_device,
        mesh=mesh,
        in_specs=(
            P(None, ("seq", "head"), None),
            P(None, "seq", "head"),
            P(None, "seq", "head"),
            P(None, "head", "seq"),
            P(None, "seq", "head"),
            P("seq", "head", None),
            P("seq", None, "head"),
            P("seq", None, "head"),
            P("seq", "head", None),
            P("seq", None, "head"),
            P(),
            P("seq"),
        ),
        out_specs=(
            P(None, "seq", "head"),
            P(None, ("seq", "head"), None),
            P(None, "seq", "head"),
            P(None, "seq", "head"),
            P(None, "head", "seq"),
            P("seq", None, "head"),
            P("seq", "head", None),
            P("seq", None, "head"),
            P("seq", None, "head"),
            P("seq", "head", None),
        ),
        check_vma=False,
    )
```

```python
from functools import partial

import jax
import jax.numpy as jnp
from jax import lax
from jax.experimental import pallas as pl
from jax.experimental.pallas import tpu as pltpu
from jax.sharding import PartitionSpec as P

HEAD_DIM = 64
STATE = 128
BLOCK = 256
F32 = jnp.float32
BF16 = jnp.bfloat16
NN = (((1,), (0,)), ((), ()))
NT = (((1,), (1,)), ((), ()))
TN = (((0,), (0,)), ((), ()))
PARAMS = pltpu.CompilerParams(vmem_limit_bytes=56 * 1024 * 1024)


def mm(a, b, dims):
    return lax.dot_general(a, b, dims, preferred_element_type=F32)


def two_term(value):
    high = value.astype(BF16)
    return high, (value - high.astype(F32)).astype(BF16)


def three_term(value):
    high, rest = value.astype(BF16), value - value.astype(BF16).astype(F32)
    middle = rest.astype(BF16)
    return high, middle, (rest - middle.astype(F32)).astype(BF16)


def mm_ones(value, ones, dims, swap=False):
    total = 0.0
    for term in three_term(value)[::-1]:
        total = total + (mm(ones, term, dims) if swap else mm(term, ones, dims))
    return total


def triangle(size, lower=True):
    row = lax.broadcasted_iota(jnp.int32, (size, size), 0)
    column = lax.broadcasted_iota(jnp.int32, (size, size), 1)
    return jnp.where(row >= column if lower else row < column, 1.0, 0.0).astype(BF16)


def running_columns(decay):
    return mm_ones(decay, triangle(decay.shape[1]), NT, True)


def spread_heads(columns, heads):
    row = lax.broadcasted_iota(jnp.int32, (heads, heads * HEAD_DIM), 0)
    lane = lax.broadcasted_iota(jnp.int32, (heads, heads * HEAD_DIM), 1)
    pick = jnp.where(lane // HEAD_DIM == row, 1.0, 0.0).astype(BF16)
    high, low = two_term(columns)
    return mm(high, pick, NN) + mm(low, pick, NN)


def head_sums(value, heads):
    width = value.shape[1]
    row = lax.broadcasted_iota(jnp.int32, (heads, width), 0)
    lane = lax.broadcasted_iota(jnp.int32, (heads, width), 1)
    pick = jnp.where(lane // HEAD_DIM == row, 1.0, 0.0).astype(BF16)
    high, low = two_term(value)
    return mm(pick, high, NT) + mm(pick, low, NT)


def masked_rows(dy, limit):
    row = lax.broadcasted_iota(jnp.int32, dy.shape, 0)
    return jnp.where(row < limit, dy.astype(F32), 0.0)


def deal_rows(state, place, outs, scratch):
    scratch[...] = state.reshape(scratch.shape)
    for k, out in enumerate(outs):
        out[0] = scratch[place ^ k].astype(BF16)


def start_grad_kernel(limits, place, dy_ref, read_ref, decay_ref, *rest):
    heads = decay_ref.shape[1]
    dy = masked_rows(dy_ref[0], limits[pl.program_id(0)])
    er = spread_heads(jnp.exp(running_columns(decay_ref[0])), heads)
    edy = (er * dy).astype(BF16)
    deal_rows(mm(read_ref[0], edy, TN), place[0], rest[:-1], rest[-1])


def local_end_kernel(place, x_ref, write_ref, decay_ref, *rest):
    heads = decay_ref.shape[1]
    x = x_ref[:, 0].reshape(-1, x_ref.shape[3])
    r = running_columns(decay_ref[0])
    ec = spread_heads(jnp.exp(r[-1:] - r), heads)
    w = (ec * x.astype(F32)).astype(BF16)
    deal_rows(mm(write_ref[0], w, TN), place[0], rest[:-1], rest[-1])


def inside_kernel(
    limits, x_ref, dy_ref, write_ref, read_ref, decay_ref, y_ref, dx_ref, dw_ref, dr_ref, sum_ref, ds_ref, dy_scr
):
    heads = decay_ref.shape[1]
    length = decay_ref.shape[2]
    decay = decay_ref[0]
    write, read = write_ref[0], read_ref[0]
    dy_scr[...] = masked_rows(dy_ref[0], limits[pl.program_id(0)]).astype(BF16)
    tri = triangle(length)
    r_col = mm_ones(decay, tri, NT, True)
    r_row = mm_ones(decay, tri, NT)
    scores = mm(read, write, NT)
    causal = lax.broadcasted_iota(jnp.int32, (length, length), 0) >= lax.broadcasted_iota(
        jnp.int32, (length, length), 1
    )
    lane = lax.broadcasted_iota(jnp.int32, (1, 2 * HEAD_DIM), 1)
    half = (
        jnp.where(lane < HEAD_DIM, 1.0, 0.0).astype(BF16),
        jnp.where(lane < HEAD_DIM, 0.0, 1.0).astype(BF16),
    )
    sums = jnp.zeros((heads, length), F32)
    row_id = lax.broadcasted_iota(jnp.int32, (heads, 2 * HEAD_DIM), 0)
    lane_id = lax.broadcasted_iota(jnp.int32, (heads, 2 * HEAD_DIM), 1)
    for pair in range(heads // 2):
        columns = slice(pair * 2 * HEAD_DIM, (pair + 1) * 2 * HEAD_DIM)
        x = x_ref[:, 0, :, columns].reshape(length, 2 * HEAD_DIM)
        dy = dy_scr[:, columns]
        y = jnp.zeros((length, 2 * HEAD_DIM), F32)
        dx = jnp.zeros((length, 2 * HEAD_DIM), F32)
        for one in range(2):
            head = pair * 2 + one
            x_one, dy_one = x * half[one], dy * half[one]
            gap = r_col[:, head : head + 1] - r_row[head : head + 1, :]
            weights = jnp.exp(jnp.where(causal, gap, -1e30))
            mixing = (weights * scores).astype(BF16)
            y = y + mm(mixing, x_one, NN)
            dx = dx + mm(mixing, dy_one, TN)
            pulled = mm(dy_one, x, NT) * weights
            if head == 0:
                ds_ref[...] = pulled
            else:
                ds_ref[...] += pulled
        y_ref[0, :, columns] = y.astype(BF16)
        dx_ref[:, 0, :, columns] = dx.astype(BF16).reshape(dx_ref.shape[0], dx_ref.shape[2], 2 * HEAD_DIM)
        pick = jnp.where(row_id == 2 * pair + lane_id // HEAD_DIM, 1.0, 0.0).astype(BF16)
        high, low = two_term(dy.astype(F32) * y - x.astype(F32) * dx)
        sums = sums + mm(pick, high, NT) + mm(pick, low, NT)
    sum_ref[0] = sums
    ds = ds_ref[...].astype(BF16)
    dr_ref[0] = mm(ds, write, NN).astype(dr_ref.dtype)
    dw_ref[0] = mm(ds, read, TN).astype(dw_ref.dtype)


class Side:
    def __init__(self, owner, place, refs, held, totals, prompts, answers):
        half = len(refs) // 4
        factors, ends, grads, seeds = (refs[k * half : (k + 1) * half] for k in range(4))
        self.half, self.prompts, self.answers = half, prompts, answers
        self.owner, self.side = owner, place[1]
        self.totals, self.held = totals, held
        for k in range(half):
            spot = place[0] ^ k
            totals[spot] = factors[k][...]
            held[spot, :prompts] = ends[k][...].astype(F32)
            held[spot, prompts : 2 * prompts] = grads[k][...].astype(F32)
            held[spot, 2 * prompts :] = seeds[k][...].astype(F32)

    def factor(self, j, prompt):
        return self.totals[j, prompt : prompt + 1, :]

    def product(self, prompt):
        result = self.factor(0, prompt)
        for j in range(1, self.half):
            result = result * self.factor(j, prompt)
        return result

    def forward(self, prompt, carried, out=None):
        for j in range(self.half):
            if out is not None:
                out[j, prompt] = carried
            carried = self.factor(j, prompt) * carried + self.held[j, prompt]
        return carried

    def backward(self, prompt, carried, out=None):
        for j in range(self.half - 1, -1, -1):
            if out is not None:
                out[j, self.prompts + prompt] = carried
            carried = self.factor(j, prompt) * carried + self.held[j, self.prompts + prompt]
        return carried

    def owner_of(self, j, answer):
        return self.owner[(self.side * self.half + j) * self.answers + answer]

    def seed(self, prompt):
        carried = jnp.zeros(self.held.shape[2:], F32)
        for j in range(self.half):
            for answer in range(self.answers):
                mine = self.held[j, 2 * self.prompts + answer]
                carried = carried + jnp.where(self.owner_of(j, answer) == prompt, mine, 0.0)
        return carried


def meet_kernel(owner, place, *rest, half, prompts, answers):
    out_ref, product_ref, held, totals = rest[4 * half :]
    here = Side(owner, place, rest[: 4 * half], held, totals, prompts, answers)
    blank = jnp.zeros(held.shape[2:], F32)
    for prompt in range(prompts):
        out_ref[prompt] = here.forward(prompt, blank).astype(BF16)
        product_ref[prompt : prompt + 1, :] = here.product(prompt)
        seed = here.seed(prompt)
        folded = here.backward(prompt, seed)
        out_ref[prompts + prompt] = jnp.where(here.side == 1, folded, seed).astype(BF16)


def chain_kernel(owner, place, met_ref, product_ref, *rest, half, prompts, answers):
    outs, answer_outs = rest[4 * half : 5 * half], rest[5 * half : 6 * half]
    held, totals, done = rest[6 * half :]
    here = Side(owner, place, rest[: 4 * half], held, totals, prompts, answers)
    finals = []
    for prompt in range(prompts):
        other = met_ref[prompt].astype(F32)
        beyond = product_ref[prompt : prompt + 1, :]
        last = here.forward(prompt, jnp.where(here.side == 1, other, 0.0), done)
        finals.append(jnp.where(here.side == 1, last, beyond * last + other))
        pull = met_ref[prompts + prompt].astype(F32)
        scale = jnp.where(here.side == 1, jnp.ones_like(beyond), beyond)
        here.backward(prompt, pull + scale * here.seed(prompt), done)
    for j in range(half):
        for answer in range(answers):
            mine = here.owner_of(j, answer)
            chosen = finals[0]
            for prompt in range(1, prompts):
                chosen = jnp.where(mine == prompt, finals[prompt], chosen)
            done[j, 2 * prompts + answer] = chosen
    for k in range(half):
        outs[k][...] = done[place[0] ^ k, : 2 * prompts].astype(BF16)
        answer_outs[k][...] = done[place[0] ^ k, 2 * prompts :].astype(BF16)


def gather_rows(place, refs, scratch):
    for k, ref in enumerate(refs):
        scratch[place ^ k] = ref[0].astype(F32)
    return scratch[...].reshape(STATE, scratch.shape[2]).astype(BF16)


def reverse_sums(value):
    return mm_ones(value, triangle(value.shape[1]), NN)


def prompt_final_kernel(place, *refs, half):
    (
        x_ref, dy_ref, write_ref, read_ref, decay_ref, yin_ref, dxin_ref, dwin_ref, drin_ref, sumin_ref,
        y_ref, dx_ref, dw_ref, dr_ref, dd_ref, scratch,
    ) = refs[2 * half :]
    heads = decay_ref.shape[1]
    start = gather_rows(place[0], refs[:half], scratch)
    grad = gather_rows(place[0], refs[half : 2 * half], scratch)
    x = x_ref[:, 0].reshape(-1, x_ref.shape[3])
    dy = dy_ref[0].astype(F32)
    write, read = write_ref[0], read_ref[0]
    r = running_columns(decay_ref[0])
    er = spread_heads(jnp.exp(r), heads)
    outside = er * mm(read, start, NN)
    y_ref[0] = (yin_ref[0].astype(F32) + outside).astype(BF16)
    dr_ref[0] = (drin_ref[0] + mm((er * dy).astype(BF16), start, NT)).astype(BF16)
    sums = sumin_ref[0] + head_sums(dy * outside, heads)
    ec = spread_heads(jnp.exp(r[-1:] - r), heads)
    xf = x.astype(F32)
    dw_ref[0] = (dwin_ref[0] + mm((ec * xf).astype(BF16), grad, NT)).astype(BF16)
    moved = ec * mm(write, grad, NN)
    dx_in = dxin_ref[:, 0].reshape(x.shape).astype(F32)
    dx_ref[:, 0] = (dx_in + moved).astype(BF16).reshape(dx_ref.shape[0], dx_ref.shape[2], dx_ref.shape[3])
    pulled = head_sums(xf * moved, heads)
    kept = head_sums(start.astype(F32) * grad.astype(F32), heads)
    closing = jnp.exp(jnp.sum(decay_ref[0], axis=1, keepdims=True)) * jnp.sum(kept, axis=1, keepdims=True)
    size = sums.shape[1]
    dd_ref[0] = reverse_sums(sums) + mm_ones(pulled, triangle(size, False), NN) + closing


def answer_final_kernel(limits, place, *refs, half):
    dy_ref, read_ref, decay_ref, yin_ref, drin_ref, sumin_ref, y_ref, dr_ref, dd_ref, scratch = refs[half:]
    heads = decay_ref.shape[1]
    limit = limits[pl.program_id(0)]
    start = gather_rows(place[0], refs[:half], scratch)
    dy = masked_rows(dy_ref[0], limit)
    er = spread_heads(jnp.exp(running_columns(decay_ref[0])), heads)
    outside = er * mm(read_ref[0], start, NN)
    y_ref[0] = masked_rows(yin_ref[0].astype(F32) + outside, limit).astype(BF16)
    dr_ref[0] = (drin_ref[0] + mm((er * dy).astype(BF16), start, NT)).astype(BF16)
    dd_ref[0] = reverse_sums(sumin_ref[0] + head_sums(dy * outside, heads))


def per_device(
    prompt_tokens,
    prompt_write,
    prompt_read,
    prompt_decay,
    prompt_cotangent,
    answer_tokens,
    answer_write,
    answer_read,
    answer_decay,
    answer_cotangent,
    group_sizes,
    answer_lengths,
):
    prompts, local_heads, length = prompt_decay.shape
    answers = answer_decay.shape[0]
    groups = prompt_write.shape[2] // STATE
    heads = local_heads // groups
    devices = lax.axis_size("seq")
    split = lax.axis_size("head")
    half = devices // 2
    position = lax.axis_index("seq")
    width, columns = heads * HEAD_DIM, local_heads * HEAD_DIM
    rows, piece = STATE // half, length // split
    assert length == BLOCK and answer_decay.shape[2] == length
    assert half & (half - 1) == 0

    token = pl.BlockSpec((split, 1, piece, width), lambda s, g, *_: (0, s, 0, g))
    wide = pl.BlockSpec((1, length, width), lambda s, g, *_: (s, 0, g))
    narrow = pl.BlockSpec((1, length, STATE), lambda s, g, *_: (s, 0, g))
    perhead = pl.BlockSpec((1, heads, length), lambda s, g, *_: (s, g, 0))

    def state_at(first):
        return [pl.BlockSpec((1, rows, width), lambda s, g, *_: (s + first, 0, g))] * half

    def shape(dims, kind=BF16):
        return jax.ShapeDtypeStruct(dims, kind)

    def call(kernel, count, prefetch, ins, outs, out_shape, name, flops, scratch=(), grid=None):
        return pl.pallas_call(
            kernel,
            grid_spec=pltpu.PrefetchScalarGridSpec(
                num_scalar_prefetch=prefetch,
                grid=grid or (count, groups),
                in_specs=ins,
                out_specs=outs,
                scratch_shapes=list(scratch),
            ),
            out_shape=out_shape,
            compiler_params=PARAMS,
            name=name,
            cost_estimate=pl.CostEstimate(
                flops=flops * count, bytes_accessed=flops * count // 200, transcendentals=0
            ),
        )

    def after(value, *others):
        return lax.optimization_barrier((value,) + others)[0]

    def deal(parts):
        return [parts[0]] + [
            lax.ppermute(parts[k], "seq", [(d, d ^ k) for d in range(devices)]) for k in range(1, half)
        ]

    def token_out(tokens):
        count = tokens.shape[0]
        packed = tokens.reshape(count, piece, split, columns).transpose(2, 0, 1, 3)
        return lax.all_to_all(packed, "head", split_axis=0, concat_axis=0, tiled=True)

    whole = jnp.full((prompts,), length, jnp.int32)
    place = jnp.stack([position % half, position // half]).astype(jnp.int32)
    state_flops = 2 * length * STATE * columns
    rows_scratch = (pltpu.VMEM((half, rows, width), F32),)

    p_x = token_out(prompt_tokens)

    total = jnp.repeat(jnp.exp(jnp.sum(prompt_decay, axis=2)), HEAD_DIM, axis=1)

    def start_grad(count, limits, dy, read, decay, name):
        return call(
            start_grad_kernel, count, 2, [wide, narrow, perhead], state_at(0),
            [shape((count, rows, columns))] * half, name, state_flops, rows_scratch,
        )(limits, place, dy, read, decay)

    grads = deal(start_grad(prompts, whole, prompt_cotangent, prompt_read, prompt_decay, "grad_prompt"))
    seeds = deal(start_grad(answers, answer_lengths, answer_cotangent, answer_read, answer_decay, "grad_answer"))
    a_x = token_out(after(answer_tokens, grads[0], seeds[0]))
    factors = deal([after(total, grads[0], seeds[0])] * half)
    local_ends = call(
        local_end_kernel, prompts, 1, [token, narrow, perhead], state_at(0),
        [shape((prompts, rows, columns))] * half, "end_prompt", state_flops, rows_scratch,
    )(place, p_x, prompt_write, prompt_decay)
    ends = deal(local_ends)

    def inside(count, limits, x, dy, write, read, decay, kind, name):
        return call(
            inside_kernel, count, 1, [token, wide, narrow, narrow, perhead],
            [wide, token, narrow, narrow, perhead],
            [
                shape((count, length, columns)),
                shape((split, count, piece, columns)),
                shape((count, length, groups * STATE), kind),
                shape((count, length, groups * STATE), F32),
                shape((count, local_heads, length), F32),
            ],
            name, 8 * length * length * columns,
            (pltpu.VMEM((length, length), F32), pltpu.VMEM((length, width), BF16)),
        )(limits, x, dy, write, read, decay)

    p_y, p_dx, p_dw, p_dr, p_sum = inside(
        prompts, after(whole, local_ends[0]), p_x, prompt_cotangent, prompt_write, prompt_read, prompt_decay, F32,
        "inside_prompt",
    )

    slots = jnp.arange(devices * answers, dtype=jnp.int32)
    bounds = jnp.cumsum(group_sizes)
    owner = jnp.sum((slots[:, None] >= bounds[None, :]).astype(jnp.int32), axis=1)
    states = 2 * prompts + answers
    lanes = 512 if columns % 512 == 0 else columns

    def strip(*dims):
        return pl.BlockSpec(dims + (lanes,), lambda c, *_: (0,) * len(dims) + (c,))

    held = pltpu.VMEM((half, states, rows, lanes), F32)
    factor_scratch = pltpu.VMEM((half, prompts, lanes), F32)
    given = [strip(prompts)] * half + [strip(prompts, rows)] * (2 * half) + [strip(answers, rows)] * half
    sizes = dict(half=half, prompts=prompts, answers=answers)
    meeting, product = call(
        partial(meet_kernel, **sizes), 1, 2, given, [strip(2 * prompts, rows), strip(prompts)],
        [shape((2 * prompts, rows, columns)), shape((prompts, columns), F32)], "meet", state_flops // 8, (held, factor_scratch), (columns // lanes,),
    )(after(owner, p_sum), place, *factors, *ends, *grads, *seeds)
    across = [(d, (d + half) % devices) for d in range(devices)]
    met, product = lax.ppermute(meeting, "seq", across), lax.ppermute(product, "seq", across)

    a_y, a_dx, a_dw, a_dr, a_sum = inside(
        answers, after(answer_lengths, meeting), a_x, answer_cotangent, answer_write, answer_read, answer_decay, BF16,
        "inside_answer",
    )

    replies = call(
        partial(chain_kernel, **sizes), 1, 2, [strip(2 * prompts, rows), strip(prompts)] + given,
        [strip(2 * prompts, rows)] * half + [strip(answers, rows)] * half,
        [shape((2 * prompts, rows, columns))] * half + [shape((answers, rows, columns))] * half,
        "chain", state_flops // 8, (held, factor_scratch, held), (columns // lanes,),
    )(after(owner, a_sum), place, met, product, *factors, *ends, *grads, *seeds)
    carried, answer_carried = deal(replies[:half]), deal(replies[half:])

    prompt_output, dx, prompt_dw, prompt_dr, prompt_dd = call(
        partial(prompt_final_kernel, half=half), prompts, 1,
        state_at(0) + state_at(prompts)
        + [token, wide, narrow, narrow, perhead, wide, token, narrow, narrow, perhead],
        [wide, token, narrow, narrow, perhead],
        [
            shape((prompts, length, columns)),
            shape((split, prompts, piece, columns)),
            shape((prompts, length, groups * STATE)),
            shape((prompts, length, groups * STATE)),
            shape((prompts, local_heads, length), F32),
        ],
        "prompt_final", 4 * state_flops, rows_scratch,
    )(place, *carried, *carried, p_x, prompt_cotangent, prompt_write, prompt_read, prompt_decay, p_y, p_dx, p_dw, p_dr, p_sum)
    answer_output, answer_dr, answer_dd = call(
        partial(answer_final_kernel, half=half), answers, 2,
        state_at(0) + [wide, narrow, perhead, wide, narrow, perhead],
        [wide, narrow, perhead],
        [
            shape((answers, length, columns)),
            shape((answers, length, groups * STATE)),
            shape((answers, local_heads, length), F32),
        ],
        "answer_final", 2 * state_flops, rows_scratch,
    )(answer_lengths, place, *answer_carried, answer_cotangent, answer_read, answer_decay, a_y, a_dr, a_sum)

    def token_back(value):
        back = lax.all_to_all(value, "head", split_axis=0, concat_axis=0, tiled=True)
        return back.transpose(1, 2, 0, 3).reshape(value.shape[1], piece, split * columns)

    return (
        prompt_output,
        token_back(dx),
        prompt_dw,
        prompt_dr,
        prompt_dd,
        answer_output,
        token_back(a_dx),
        a_dw,
        answer_dr,
        answer_dd,
    )


def solution(mesh):
    return jax.shard_map(
        per_device,
        mesh=mesh,
        in_specs=(
            P(None, ("seq", "head"), None),
            P(None, "seq", "head"),
            P(None, "seq", "head"),
            P(None, "head", "seq"),
            P(None, "seq", "head"),
            P("seq", "head", None),
            P("seq", None, "head"),
            P("seq", None, "head"),
            P("seq", "head", None),
            P("seq", None, "head"),
            P(),
            P("seq"),
        ),
        out_specs=(
            P(None, "seq", "head"),
            P(None, ("seq", "head"), None),
            P(None, "seq", "head"),
            P(None, "seq", "head"),
            P(None, "head", "seq"),
            P("seq", None, "head"),
            P("seq", "head", None),
            P("seq", None, "head"),
            P("seq", None, "head"),
            P("seq", "head", None),
        ),
        check_vma=False,
    )
```
